512 devices in a mesh: rows: 64 (over y, z), sub: 8 (over x, core).
Axes of the slice: x: 4, y: 4, z: 16, core: 2. Of those that a mesh axis runs over, the one named last changes fastest.
Arguments:
- affinity: bfloat16 [4096, 3, 256, 256], P(('rows', 'sub')), may hold values from 0.0099487305 to 1
- old_basis: bfloat16 [1048576, 64], P(('rows', 'sub')), may hold values from -1500 to 1500, as said below
- degrees: int32 [1048576], P(('rows', 'sub')), may hold values from 10 to 90
- column_blocks: int32 [4096, 3], P(('rows', 'sub')), may hold values from 0 to 4095, as said below
- reorder: int32 [4096, 256], P(('rows', 'sub')), may hold values from 0 to 255, each once within a row
Outputs:
- targets: float32 [1048576, 64], P(('rows', 'sub'))
The draws below stay inside these ranges and needn't reach their ends.
Inputs may be any that keep to these rules, and one draw needn't show every extreme that they name: column_blocks[b, 0] = b; the other entries of row b are distinct, differ from b and lie within 2 of b; block row 0 names block 2. `old_basis`: entries of magnitude up to 1500.
All inputs are finite; a program needn't handle non-finite values.
Results may differ from the reference program's by a relative error of at most 0.0035.
Values may be sent and summed in bfloat16 or wider, within the bound.
A program may use at most 64 MiB of HBM per device.

```python
import math
import jax
import jax.numpy as jnp
from jax import lax

BLK = 256
RANK = 64
NB = 3
REACH = 2
NBLK = 4096
ITEMS = 1048576


def draw_column_blocks(key, part):
    offsets = jnp.concatenate([jnp.arange(-REACH, 0, dtype=jnp.int32), jnp.arange(1, REACH + 1, dtype=jnp.int32)])
    spread = 2 * REACH
    row_ids = jnp.arange(NBLK, dtype=jnp.int32)[:, None]
    candidates = row_ids + offsets[None, :]
    invalid = ((candidates < 0) | (candidates >= NBLK)).astype(jnp.int32)
    scores = jax.random.randint(key, (NBLK, spread), 0, 1 << 20, dtype=jnp.int32) * spread
    scores = scores + jnp.arange(spread, dtype=jnp.int32)[None, :] + invalid * (1 << 28)
    order = jnp.argsort(scores, axis=1, stable=True)
    chosen = jnp.take_along_axis(candidates, order[:, :NB - 1], axis=1)
    return jnp.concatenate([row_ids, chosen], axis=1).astype(jnp.int32)


def draw_old_basis(key, part):
    first_key, second_key, third_key = jax.random.split(jax.random.fold_in(key, 7), 3)
    position = jnp.arange(ITEMS, dtype=jnp.float32)[:, None] / ITEMS
    row_scale = 10.0 ** jax.random.uniform(second_key, (ITEMS, 1), jnp.float32)
    column_scale = 10.0 ** jax.random.uniform(third_key, (1, RANK), jnp.float32)
    base = jnp.clip(jax.random.normal(first_key, (ITEMS, RANK), jnp.float32), -5.0, 5.0)
    trend = 1.7320508 ** position
    return (base * row_scale * column_scale * trend).astype(jnp.bfloat16)


def place_ends(values, own_key, least, largest):
    longest = values.shape.index(max(values.shape))
    spots = []
    for shift in (0, 1):
        where = [jax.random.randint(jax.random.fold_in(own_key, axis), (), 0, length) for axis, length in enumerate(values.shape)]
        where[longest] = (where[longest] + shift) % values.shape[longest]
        spots.append(tuple(where))
    return values.at[spots[0]].set(least).at[spots[1]].set(largest)


def block_levels(rng, extent, pieces, least, high):
    loudness = 1.0
    for dim, parts in pieces:
        draws = jax.random.uniform(jax.random.fold_in(jax.random.fold_in(rng, 6), dim), (parts,), jnp.float32, least / len(pieces), high / len(pieces))
        loudness = loudness * jnp.repeat(jnp.exp(draws), extent[dim] // parts).reshape((-1,) + (1,) * (len(extent) - 1 - dim))
    return loudness


def setup_inputs(seed: int = 0) -> dict:
    keys = jax.random.split(jax.random.key(seed), 6)
    affinity = jnp.clip(jnp.exp(math.log(1.0) - 4.61031033 * jax.random.uniform(keys[0], (NBLK, NB, BLK, BLK), jnp.float32) ** block_levels(keys[0], (NBLK, NB, BLK, BLK), ((0, 512),), -0.2, 0.2)), 0.0099487305, 1.0).astype(jnp.bfloat16)
    old_basis = draw_old_basis(jax.random.fold_in(keys[5], 71), 0)
    degrees = place_ends(jax.random.randint(keys[2], (ITEMS,), 10, 91), jax.random.fold_in(keys[2], 1), 10, 90).astype(jnp.int32)
    column_blocks = draw_column_blocks(jax.random.fold_in(keys[5], 71), 0)
    reorder = jax.vmap(lambda own: jax.random.permutation(own, BLK))(jax.random.split(keys[4], NBLK)).reshape((NBLK, BLK)).astype(jnp.int32)
    return dict(affinity=affinity, old_basis=old_basis, degrees=degrees, column_blocks=column_blocks, reorder=reorder)


def reference(affinity, old_basis, degrees, column_blocks, reorder):
    inverse_root = lax.rsqrt(degrees.astype(jnp.float32))[:, None]
    scaled = (inverse_root * old_basis.astype(jnp.float32)).astype(jnp.bfloat16)
    blocks = scaled.reshape(NBLK, BLK, RANK)

    def block_row(pair):
        aff_row, col_row = pair
        picked = blocks[col_row]
        total = jnp.zeros((BLK, RANK), jnp.float32)
        for slot in range(NB):
            total = total + jnp.dot(aff_row[slot].astype(jnp.float32), picked[slot].astype(jnp.float32), preferred_element_type=jnp.float32)
        return total
    product = lax.map(block_row, (affinity, column_blocks))
    image_rows = product.reshape(ITEMS, RANK) * inverse_root
    gram = jnp.dot(image_rows.T.astype(jnp.float32), image_rows.astype(jnp.float32), precision=lax.Precision.HIGHEST, preferred_element_type=jnp.float32)
    lower = jnp.linalg.cholesky(gram)
    solved = lax.linalg.triangular_solve(lower, image_rows.T, left_side=True, lower=True)
    clustered = (solved.T * jnp.sqrt(jnp.float32(ITEMS))).reshape(NBLK, BLK, RANK)
    targets = jnp.take_along_axis(clustered, reorder[:, :, None], axis=1)
    return targets.reshape(ITEMS, RANK)
```

```python
import functools
import math

import jax
import jax.numpy as jnp
from jax import lax
from jax.experimental import pallas as pl
from jax.experimental.pallas import tpu as pltpu
from jax.sharding import PartitionSpec as P

MESH = pl.DeviceIdType.MESH
REACH = 2
NT = (((1,), (1,)), ((), ()))
F32 = jnp.float32
BF16 = jnp.bfloat16


def dot(a, b):
    return jnp.dot(a, b, preferred_element_type=F32)


def dot_nt(a, b):
    return lax.dot_general(a, b, NT, preferred_element_type=F32)


def front_kernel(
    dims,
    cols_ref, aff_hbm, basis_hbm, deg_hbm, reorder_hbm,
    gram_out, perm_out,
    aff, basis, deg, reorder, own, ext, iroot, acc0, parts,
    gpack, rs_buf, z_src, z_buf, ag_src, ag_buf,
    in_sem, aff_sem, halo_send, halo_recv, rs_send, rs_recv, z_send, z_recv, ag_send, ag_recv, out_sem,
):
    nz, ny, ns, count, block = dims
    plane = ny * ns
    total = plane * nz
    row, sub = lax.axis_index("rows"), lax.axis_index("sub")
    y, z = row // nz, row % nz
    mine = y * ns + sub
    linear = row * ns + sub

    def plane_id(q):
        return ((q // ns) * nz + z, q % ns)

    def z_id(w):
        return (y * nz + w, sub)

    def line_id(i):
        return (i // ns, i % ns)

    right = line_id((linear + 1) % total)
    left = line_id((linear + total - 1) % total)

    barrier = pltpu.get_barrier_semaphore()

    def signal(device):
        pl.semaphore_signal(barrier, inc=1, device_id=device, device_id_type=MESH)

    signal(left)
    signal(right)

    @pl.loop(1, nz)
    def _(d):
        signal(z_id((z + d) % nz))

    @pl.loop(1, plane)
    def _(d):
        signal(plane_id((mine + d) % plane))

    basis_in = pltpu.make_async_copy(basis_hbm, basis, in_sem.at[0])
    deg_in = pltpu.make_async_copy(deg_hbm, deg, in_sem.at[1])
    reorder_in = pltpu.make_async_copy(reorder_hbm, reorder, in_sem.at[2])
    deg_in.start()
    basis_in.start()

    def aff_in(b):
        return pltpu.make_async_copy(aff_hbm.at[b], aff.at[b], aff_sem.at[b])

    inner = tuple(range(REACH, count - REACH))
    outer = tuple(range(REACH)) + tuple(range(count - REACH, count))
    for b in inner + outer:
        aff_in(b).start()
    reorder_in.start()

    deg_in.wait()
    root = lax.rsqrt(deg[...].astype(F32))
    for b in range(count):
        for h in range(block // 128):
            r = b * (block // 128) + h
            iroot[b, :, h * 128 : (h + 1) * 128] = root[r : r + 1, :]
    basis_in.wait()
    for b in range(count):
        s = (basis[:, b * block : (b + 1) * block].astype(F32) * iroot[b]).astype(BF16)
        own[b] = s
        ext[b + REACH] = s

    pl.semaphore_wait(barrier, 2 + (nz - 1) + (plane - 1))

    to_right = pltpu.make_async_remote_copy(
        own.at[pl.ds(count - REACH, REACH)], ext.at[pl.ds(0, REACH)],
        halo_send.at[0], halo_recv.at[0], device_id=right, device_id_type=MESH)
    to_left = pltpu.make_async_remote_copy(
        own.at[pl.ds(0, REACH)], ext.at[pl.ds(count + REACH, REACH)],
        halo_send.at[1], halo_recv.at[1], device_id=left, device_id_type=MESH)
    to_right.start()
    to_left.start()

    first = linear * count

    def finish(b, acc, gram):
        image = acc * iroot[b]
        hi = image.astype(BF16)
        rest = image - hi.astype(F32)
        mid = rest.astype(BF16)
        lo = (rest - mid.astype(F32)).astype(BF16)
        rank = hi.shape[0]
        parts[b, :rank, :] = hi
        parts[b, rank:, :] = mid
        g1 = dot_nt(jnp.concatenate([hi, mid, lo], axis=0), hi)
        g2 = dot_nt(jnp.concatenate([hi, mid], axis=0), mid)
        g3 = dot_nt(hi, lo)
        small = g1[2 * rank :] + g2[rank:] + g3
        cross = g1[rank : 2 * rank] + g2[:rank]
        return gram + (g1[:rank] + (cross + small))

    rank = basis.shape[0]

    def early(b, gram):
        aff_in(b).wait()
        acc = dot_nt(own[b], aff[b, 0])
        for k in range(1, 3):
            acc += dot_nt(own[jnp.clip(cols_ref[k, b] - first, 0, count - 1)], aff[b, k])
        return finish(b, acc, gram)

    gram = lax.fori_loop(REACH, count - REACH, early, jnp.zeros((rank, rank), F32))

    def outer_block(j):
        return j + (count - 2 * REACH) * (j // REACH)

    @pl.loop(0, 2 * REACH)
    def _(j):
        b = outer_block(j)
        aff_in(b).wait()
        acc0[j] = dot_nt(own[b], aff[b, 0])

    to_right.wait()
    to_left.wait()

    def late(j, gram):
        b = outer_block(j)
        acc = acc0[j]
        for k in range(1, 3):
            acc += dot_nt(ext[jnp.clip(cols_ref[k, b] - first + REACH, 0, count + 2 * REACH - 1)], aff[b, k])
        return finish(b, acc, gram)

    gram = lax.fori_loop(0, 2 * REACH, late, gram)

    half = rank // 2
    packed = jnp.concatenate([gram[:half], gram[half:]], axis=1)
    per = half // plane
    for q in range(plane):
        gpack[q] = packed[q * per : (q + 1) * per]

    def rs_copy(d):
        q = (mine + d) % plane
        return pltpu.make_async_remote_copy(
            gpack.at[q], rs_buf.at[d - 1], rs_send.at[d - 1], rs_recv.at[d - 1],
            device_id=plane_id(q), device_id_type=MESH)

    def z_copy(d):
        return pltpu.make_async_remote_copy(
            z_src, z_buf.at[d - 1], z_send.at[d - 1], z_recv.at[d - 1],
            device_id=z_id((z + d) % nz), device_id_type=MESH)

    def ag_copy(d):
        q = (mine + d) % plane
        return pltpu.make_async_remote_copy(
            ag_src, ag_buf.at[mine], ag_send.at[d - 1], ag_recv.at[d - 1],
            device_id=plane_id(q), device_id_type=MESH)

    @pl.loop(1, plane)
    def _(d):
        rs_copy(d).start()

    reorder_in.wait()
    ids = lax.broadcasted_iota(jnp.int32, (block, block), 0)

    @pl.loop(0, count)
    def _(b):
        pick = jnp.where(ids == reorder[pl.ds(b, 1), :], 1.0, 0.0).astype(BF16)
        parts[b] = dot(parts[b], pick).astype(BF16)

    perm_copy = pltpu.make_async_copy(parts, perm_out, out_sem)
    perm_copy.start()

    @pl.loop(1, plane)
    def _(d):
        rs_copy(d).wait_recv()

    z_src[...] = gpack[mine] + jnp.sum(rs_buf[...], axis=0)

    @pl.loop(1, nz)
    def _(d):
        z_copy(d).start()

    @pl.loop(1, plane)
    def _(d):
        rs_copy(d).wait_send()

    @pl.loop(1, nz)
    def _(d):
        z_copy(d).wait_recv()

    chunk = z_src[...] + jnp.sum(z_buf[...], axis=0)
    ag_src[...] = chunk
    ag_buf[mine] = chunk

    @pl.loop(1, plane)
    def _(d):
        ag_copy(d).start()

    @pl.loop(1, nz)
    def _(d):
        z_copy(d).wait_send()

    perm_copy.wait()

    @pl.loop(1, plane)
    def _(d):
        ag_copy(d).wait()

    for q in range(plane):
        gram_out[q * per : (q + 1) * per] = ag_buf[q]


def back_kernel(scale, gram_ref, perm_hbm, out_hbm, perm, out, in_sem, out_sem):
    count, depth, block = perm.shape
    rank = depth // 2
    half = rank // 2
    tiles = rank // 8

    def perm_in(b):
        return pltpu.make_async_copy(perm_hbm.at[b], perm.at[b], in_sem.at[b])

    for b in range(count):
        perm_in(b).start()

    packed = gram_ref[...]
    low = pltpu.roll(packed, rank, 1)
    lane = lax.broadcasted_iota(jnp.int32, (8, 2 * rank), 1)
    sublane = lax.broadcasted_iota(jnp.int32, (8, 2 * rank), 0)
    state = []
    for t in range(tiles):
        source = low if t < tiles // 2 else packed
        r = (8 * t) % half
        eye = jnp.where(lane == sublane + 8 * t, 1.0, 0.0)
        state.append(jnp.where(lane < rank, eye, source[r : r + 8]))

    def row(v, j):
        return jnp.broadcast_to(v[j : j + 1, :], v.shape)

    rows = []
    for t in range(tiles):
        cols = []
        for j in range(8):
            k = rank + 8 * t + j
            cols.append([jnp.broadcast_to(state[v][:, k : k + 1], (8, 2 * rank)) for v in range(t, tiles)])
        pivots = None
        mults = []
        pivot_rows = []
        for j in range(8):
            pivot = row(cols[j][0], j)
            pivots = pivot if pivots is None else jnp.where(sublane == j, pivot, pivots)
            inv = 1.0 / pivot
            mult = [c * inv for c in cols[j]]
            mult[0] = jnp.where(sublane > j, mult[0], 0.0)
            for jj in range(j + 1, 8):
                top = row(cols[jj][0], j)
                cols[jj] = [c - m * top for c, m in zip(cols[jj], mult)]
            pivot_row = row(state[t], j)
            state[t] = state[t] - mult[0] * pivot_row
            mults.append(mult)
            pivot_rows.append(pivot_row)
        for v in range(t + 1, tiles):
            upd = mults[0][v - t] * pivot_rows[0]
            for j in range(1, 8):
                upd = upd + mults[j][v - t] * pivot_rows[j]
            state[v] = state[v] - upd
        rows.append(state[t] * (lax.rsqrt(pivots) * scale))

    inverse = jnp.concatenate(rows, axis=0)[:, :rank]
    hi = inverse.astype(BF16)
    mid = (inverse - hi.astype(F32)).astype(BF16)
    left = jnp.concatenate(
        [jnp.concatenate([hi, hi], axis=1), jnp.concatenate([mid, mid], axis=1)], axis=0)

    def out_copy(b):
        cols = pl.ds(b * block, block)
        return pltpu.make_async_copy(out.at[:, cols], out_hbm.at[:, cols], out_sem.at[b])

    for b in range(count):
        perm_in(b).wait()
        both = dot(left, perm[b])
        out[:, b * block : (b + 1) * block] = both[:rank] + both[rank:]
        out_copy(b).start()
    for b in range(count):
        out_copy(b).wait()


def body(ny, nz, ns, affinity, old_basis, degrees, column_blocks, reorder):
    count, _, block, _ = affinity.shape
    rows_here, rank = old_basis.shape
    plane = ny * ns
    per = rank // 2 // plane
    anywhere = pl.BlockSpec(memory_space=pl.ANY)
    vmem = pl.BlockSpec(memory_space=pltpu.VMEM)
    dma = pltpu.SemaphoreType.DMA
    gram, perm = pl.pallas_call(
        functools.partial(front_kernel, (nz, ny, ns, count, block)),
        name="front",
        out_shape=(
            jax.ShapeDtypeStruct((rank // 2, 2 * rank), F32),
            jax.ShapeDtypeStruct((count, 2 * rank, block), BF16),
        ),
        in_specs=[pl.BlockSpec(memory_space=pltpu.SMEM)] + [anywhere] * 4,
        out_specs=(vmem, anywhere),
        scratch_shapes=[
            pltpu.VMEM(affinity.shape, BF16),
            pltpu.VMEM((rank, rows_here), BF16),
            pltpu.VMEM((rows_here // 128, 128), jnp.int32),
            pltpu.VMEM(reorder.shape, jnp.int32),
            pltpu.VMEM((count, rank, block), BF16),
            pltpu.VMEM((count + 2 * REACH, rank, block), BF16),
            pltpu.VMEM((count, 1, block), F32),
            pltpu.VMEM((2 * REACH, rank, block), F32),
            pltpu.VMEM((count, 2 * rank, block), BF16),
            pltpu.VMEM((plane, per, 2 * rank), F32),
            pltpu.VMEM((plane - 1, per, 2 * rank), F32),
            pltpu.VMEM((per, 2 * rank), F32),
            pltpu.VMEM((nz - 1, per, 2 * rank), F32),
            pltpu.VMEM((per, 2 * rank), F32),
            pltpu.VMEM((plane, per, 2 * rank), F32),
            dma((3,)),
            dma((count,)),
            dma((2,)),
            dma((2,)),
            dma((plane - 1,)),
            dma((plane - 1,)),
            dma((nz - 1,)),
            dma((nz - 1,)),
            dma((plane - 1,)),
            dma((plane - 1,)),
            dma,
        ],
        compiler_params=pltpu.CompilerParams(collective_id=0, has_side_effects=True),
    )(column_blocks.T, affinity, old_basis.T, degrees.reshape(-1, 128), reorder)
    items = rows_here * lax.axis_size("rows") * lax.axis_size("sub")
    out = pl.pallas_call(
        functools.partial(back_kernel, math.sqrt(items)),
        name="back",
        out_shape=jax.ShapeDtypeStruct((rank, rows_here), F32),
        in_specs=[vmem, anywhere],
        out_specs=anywhere,
        scratch_shapes=[
            pltpu.VMEM((count, 2 * rank, block), BF16),
            pltpu.VMEM((rank, rows_here), F32),
            dma((count,)),
            dma((count,)),
        ],
    )(gram, perm)
    return out.T


def solution(mesh):
    rows, ns = mesh.shape["rows"], mesh.shape["sub"]
    nz = 16 if rows % 16 == 0 else rows // 2
    both = P(("rows", "sub"))
    return jax.shard_map(
        functools.partial(body, rows // nz, nz, ns),
        mesh=mesh, in_specs=(both,) * 5, out_specs=both, check_vma=False,
    )
```

```python
import functools
import math

import jax
import jax.numpy as jnp
from jax import lax
from jax.experimental import pallas as pl
from jax.experimental.pallas import tpu as pltpu
from jax.sharding import PartitionSpec as P

MESH = pl.DeviceIdType.MESH
REACH = 2
NT = (((1,), (1,)), ((), ()))
F32 = jnp.float32
BF16 = jnp.bfloat16


def dot(a, b):
    return jnp.dot(a, b, preferred_element_type=F32)


def dot_nt(a, b):
    return lax.dot_general(a, b, NT, preferred_element_type=F32)


def wrap(value, size):
    return jnp.where(value >= size, value - size, value)


def around(offset, size):
    return min(offset, size - offset)


def front_kernel(
    dims,
    cols_hbm, aff_hbm, basis_hbm, deg_hbm, reorder_hbm,
    gram_out, perm_out,
    cols, aff, basis, deg, reorder, halo, halo_deg, ext, iroot, parts,
    gpack, rs_buf, z_src, z_buf, ag_src, ag_buf,
    in_sem, aff_sem, halo_send, halo_recv, rs_send, rs_recv, z_send, z_recv, ag_send, ag_recv,
):
    nz, ny, ns, count, block = dims
    plane = ny * ns
    total = plane * nz
    rank = basis.shape[0]
    row, sub = lax.axis_index("rows"), lax.axis_index("sub")
    y, z = row // nz, row % nz
    mine = y * ns + sub
    linear = row * ns + sub

    up, down = wrap(linear + 1, total), wrap(linear + total - 1, total)
    right = (up // ns, up % ns)
    left = (down // ns, down % ns)
    ys = [wrap(y + d, ny) for d in range(ny)]
    subs = [wrap(sub + d, ns) for d in range(ns)]
    plane_offsets = sorted(
        ((dy, ds) for dy in range(ny) for ds in range(ns) if dy or ds),
        key=lambda o: -(2 * around(o[0], ny) + around(o[1], ns)))
    plane_ids = [(ys[dy] * nz + z, subs[ds]) for dy, ds in plane_offsets]
    plane_slots = [ys[dy] * ns + subs[ds] for dy, ds in plane_offsets]
    z_offsets = sorted(range(1, nz), key=lambda d: -around(d, nz))
    z_ids = [(y * nz + wrap(z + d, nz), sub) for d in z_offsets]

    barrier = pltpu.get_barrier_semaphore()

    def signal(device):
        pl.semaphore_signal(barrier, inc=1, device_id=device, device_id_type=MESH)

    def remote(src, dst, send, recv, device):
        return pltpu.make_async_remote_copy(
            src, dst, send, recv, device_id=device, device_id_type=MESH)

    def drain(ref, sem):
        pltpu.make_async_copy(ref, ref, sem).wait()

    signal(left)
    signal(right)

    deg_in = pltpu.make_async_copy(deg_hbm, deg, in_sem.at[0])
    basis_in = pltpu.make_async_copy(basis_hbm, basis, in_sem.at[1])
    cols_in = pltpu.make_async_copy(cols_hbm, cols, in_sem.at[2])
    reorder_in = pltpu.make_async_copy(reorder_hbm, reorder, in_sem.at[3])

    def aff_in(b):
        return pltpu.make_async_copy(aff_hbm.at[b], aff.at[b], aff_sem.at[b])

    inner = tuple(range(REACH, count - REACH))
    outer = tuple(range(REACH)) + tuple(range(count - REACH, count))
    deg_in.start()
    basis_in.start()
    cols_in.start()
    for b in inner:
        aff_in(b).start()
    for device in plane_ids + z_ids:
        signal(device)
    for b in outer:
        aff_in(b).start()
    reorder_in.start()

    pl.semaphore_wait(barrier, 2 + (nz - 1) + (plane - 1))

    width = REACH * block
    pieces = deg.shape[0]
    sends = [
        remote(basis_hbm.at[:, pl.ds((count - REACH) * block, width)], halo.at[0],
               halo_send.at[0], halo_recv.at[0], right),
        remote(basis_hbm.at[:, pl.ds(0, width)], halo.at[1],
               halo_send.at[1], halo_recv.at[1], left),
        remote(deg_hbm.at[pieces - 1], halo_deg.at[0], halo_send.at[2], halo_recv.at[2], right),
        remote(deg_hbm.at[0], halo_deg.at[1], halo_send.at[3], halo_recv.at[3], left),
    ]
    for copy in sends:
        copy.start()

    def spread(root, first_row):
        return jnp.concatenate(
            [root[first_row + h : first_row + h + 1, :] for h in range(block // 128)], axis=1)

    def scaled(raw, factor):
        return (raw.astype(F32) * factor).astype(BF16)

    per_block = block // 128
    deg_in.wait()
    for g in range(pieces):
        root = lax.rsqrt(deg[g].astype(F32))
        for j in range(REACH):
            iroot[g * REACH + j] = spread(root, j * per_block)
    basis_in.wait()
    for b in range(count):
        ext[b + REACH] = scaled(basis[:, b * block : (b + 1) * block], iroot[b])
    cols_in.wait()

    first = linear * count

    def picked(k, b, low, high):
        return ext[jnp.clip(cols[k, b] - first + REACH, low, high)]

    def split(b, acc):
        image = acc * iroot[b]
        hi = image.astype(BF16)
        rest = image - hi.astype(F32)
        mid = rest.astype(BF16)
        lo = (rest - mid.astype(F32)).astype(BF16)
        parts[b, :rank, :] = hi
        parts[b, rank:, :] = mid
        return hi, mid, lo

    def gram_of(splits):
        hi, mid, lo = (jnp.concatenate(p, axis=1) for p in zip(*splits))
        g1 = dot_nt(jnp.concatenate([hi, mid, lo], axis=0), hi)
        g2 = dot_nt(jnp.concatenate([hi, mid], axis=0), mid)
        g3 = dot_nt(hi, lo)
        small = g1[2 * rank :] + g2[rank:] + g3
        cross = g1[rank : 2 * rank] + g2[:rank]
        return g1[:rank] + (cross + small)

    for b in inner:
        aff_in(b).wait()
    splits = []
    for b in inner:
        acc = dot_nt(ext[b + REACH], aff[b, 0])
        for k in range(1, 3):
            acc += dot_nt(picked(k, b, REACH, count + REACH - 1), aff[b, k])
        splits.append(split(b, acc))
    gram = gram_of(splits)
    for b in outer:
        aff_in(b).wait()
    starts = [dot_nt(ext[b + REACH], aff[b, 0]) for b in outer]

    for copy in sends:
        copy.wait_recv()
    for side, base in ((0, 0), (1, count + REACH)):
        root = lax.rsqrt(halo_deg[side].astype(F32))
        for j in range(REACH):
            ext[base + j] = scaled(
                halo[side, :, j * block : (j + 1) * block], spread(root, j * per_block))

    splits = []
    for b, acc in zip(outer, starts):
        for k in range(1, 3):
            acc += dot_nt(picked(k, b, 0, count + 2 * REACH - 1), aff[b, k])
        splits.append(split(b, acc))
    gram += gram_of(splits)

    half = rank // 2
    packed = jnp.concatenate([gram[:half], gram[half:]], axis=1)
    per = half // plane
    for q in range(plane):
        gpack[q] = packed[q * per : (q + 1) * per]

    for i, (device, q) in enumerate(zip(plane_ids, plane_slots)):
        remote(gpack.at[q], rs_buf.at[i], rs_send, rs_recv, device).start()

    reorder_in.wait()
    ids = lax.broadcasted_iota(jnp.int32, (block, block), 0)
    for b in range(count):
        pick = jnp.where(ids == reorder[b : b + 1, :], 1.0, 0.0).astype(BF16)
        perm_out[b] = dot(parts[b], pick).astype(BF16)

    drain(rs_buf, rs_recv)
    z_src[...] = gpack[mine] + jnp.sum(rs_buf[...], axis=0)
    for i, device in enumerate(z_ids):
        remote(z_src, z_buf.at[i], z_send, z_recv, device).start()
    for copy in sends:
        copy.wait_send()
    drain(rs_buf, rs_send)

    drain(z_buf, z_recv)
    chunk = z_src[...] + jnp.sum(z_buf[...], axis=0)
    ag_src[...] = chunk
    ag_buf[mine] = chunk
    for device in plane_ids:
        remote(ag_src, ag_buf.at[mine], ag_send, ag_recv, device).start()
    drain(z_buf, z_send)
    drain(ag_buf.at[pl.ds(0, plane - 1)], ag_recv)
    for q in range(plane):
        gram_out[q * per : (q + 1) * per] = ag_buf[q]
    drain(ag_buf.at[pl.ds(0, plane - 1)], ag_send)


def back_kernel(scale, gram_ref, perm, out_hbm, out, out_sem):
    count, depth, block = perm.shape
    rank = depth // 2
    half = rank // 2
    tiles = rank // 8

    packed = gram_ref[...]
    low = pltpu.roll(packed, rank, 1)
    lane = lax.broadcasted_iota(jnp.int32, (8, 2 * rank), 1)
    sublane = lax.broadcasted_iota(jnp.int32, (8, 2 * rank), 0)
    state = []
    for t in range(tiles):
        source = low if t < tiles // 2 else packed
        r = (8 * t) % half
        eye = jnp.where(lane == sublane + 8 * t, 1.0, 0.0)
        state.append(jnp.where(lane < rank, eye, source[r : r + 8]))

    def row(v, j):
        return jnp.broadcast_to(v[j : j + 1, :], v.shape)

    rows = []
    for t in range(tiles):
        cols = []
        for j in range(8):
            k = rank + 8 * t + j
            cols.append([jnp.broadcast_to(state[v][:, k : k + 1], (8, 2 * rank)) for v in range(t, tiles)])
        pivots = None
        mults = []
        pivot_rows = []
        for j in range(8):
            pivot = row(cols[j][0], j)
            pivots = pivot if pivots is None else jnp.where(sublane == j, pivot, pivots)
            inv = 1.0 / pivot
            mult = [c * inv for c in cols[j]]
            mult[0] = jnp.where(sublane > j, mult[0], 0.0)
            for jj in range(j + 1, 8):
                top = row(cols[jj][0], j)
                cols[jj] = [c - m * top for c, m in zip(cols[jj], mult)]
            pivot_row = row(state[t], j)
            state[t] = state[t] - mult[0] * pivot_row
            mults.append(mult)
            pivot_rows.append(pivot_row)
        for v in range(t + 1, tiles):
            upd = mults[0][v - t] * pivot_rows[0]
            for j in range(1, 8):
                upd = upd + mults[j][v - t] * pivot_rows[j]
            state[v] = state[v] - upd
        rows.append(state[t] * (lax.rsqrt(pivots) * scale))

    inverse = jnp.concatenate(rows, axis=0)[:, :rank]
    hi = inverse.astype(BF16)
    mid = (inverse - hi.astype(F32)).astype(BF16)
    left = jnp.concatenate(
        [jnp.concatenate([hi, hi], axis=1), jnp.concatenate([mid, mid], axis=1)], axis=0)

    def out_copy(b):
        cols = pl.ds(b * block, block)
        return pltpu.make_async_copy(out.at[:, cols], out_hbm.at[:, cols], out_sem.at[b])

    for b in range(count):
        both = dot(left, perm[b])
        out[:, b * block : (b + 1) * block] = both[:rank] + both[rank:]
        out_copy(b).start()
    for b in range(count):
        out_copy(b).wait()


def body(ny, nz, ns, affinity, old_basis, degrees, column_blocks, reorder):
    count, _, block, _ = affinity.shape
    rows_here, rank = old_basis.shape
    plane = ny * ns
    per = rank // 2 // plane
    anywhere = pl.BlockSpec(memory_space=pl.ANY)
    vmem = pl.BlockSpec(memory_space=pltpu.VMEM)
    dma = pltpu.SemaphoreType.DMA
    width = REACH * block // 128
    gram, perm = pl.pallas_call(
        functools.partial(front_kernel, (nz, ny, ns, count, block)),
        name="front",
        out_shape=(
            pltpu.VMEM((rank // 2, 2 * rank), F32),
            pltpu.VMEM((count, 2 * rank, block), BF16),
        ),
        in_specs=[anywhere] * 5,
        out_specs=(vmem, vmem),
        scratch_shapes=[
            pltpu.SMEM(column_blocks.shape[::-1], jnp.int32),
            pltpu.VMEM(affinity.shape, BF16),
            pltpu.VMEM((rank, rows_here), BF16),
            pltpu.VMEM((count // REACH, width, 128), jnp.int32),
            pltpu.VMEM(reorder.shape, jnp.int32),
            pltpu.VMEM((2, rank, REACH * block), BF16),
            pltpu.VMEM((2, width, 128), jnp.int32),
            pltpu.VMEM((count + 2 * REACH, rank, block), BF16),
            pltpu.VMEM((count, 1, block), F32),
            pltpu.VMEM((count, 2 * rank, block), BF16),
            pltpu.VMEM((plane, per, 2 * rank), F32),
            pltpu.VMEM((plane - 1, per, 2 * rank), F32),
            pltpu.VMEM((per, 2 * rank), F32),
            pltpu.VMEM((nz - 1, per, 2 * rank), F32),
            pltpu.VMEM((per, 2 * rank), F32),
            pltpu.VMEM((plane, per, 2 * rank), F32),
            dma((4,)), dma((count,)), dma((4,)), dma((4,)),
            dma, dma, dma, dma, dma, dma,
        ],
        compiler_params=pltpu.CompilerParams(collective_id=0, has_side_effects=True),
    )(column_blocks.T, affinity, old_basis.T, degrees.reshape(-1, width, 128), reorder)
    items = rows_here * lax.axis_size("rows") * lax.axis_size("sub")
    out = pl.pallas_call(
        functools.partial(back_kernel, math.sqrt(items)),
        name="back",
        out_shape=jax.ShapeDtypeStruct((rank, rows_here), F32),
        in_specs=[vmem, vmem],
        out_specs=anywhere,
        scratch_shapes=[pltpu.VMEM((rank, rows_here), F32), dma((count,))],
    )(*(pltpu.with_memory_space_constraint(a, pltpu.VMEM) for a in (gram, perm)))
    return out.T


def solution(mesh):
    rows, ns = mesh.shape["rows"], mesh.shape["sub"]
    nz = 16 if rows % 16 == 0 else rows // 2
    both = P(("rows", "sub"))
    return jax.shard_map(
        functools.partial(body, rows // nz, nz, ns),
        mesh=mesh, in_specs=(both,) * 5, out_specs=both, check_vma=False,
    )
```

```python
import functools
import math

import jax
import jax.numpy as jnp
from jax import lax
from jax.experimental import pallas as pl
from jax.experimental.pallas import tpu as pltpu
from jax.sharding import PartitionSpec as P

MESH = pl.DeviceIdType.MESH
REACH = 2
NT = (((1,), (1,)), ((), ()))
F32 = jnp.float32
BF16 = jnp.bfloat16


def dot(a, b):
    return jnp.dot(a, b, preferred_element_type=F32)


def dot_nt(a, b):
    return lax.dot_general(a, b, NT, preferred_element_type=F32)


def wrap(value, size):
    return jnp.where(value >= size, value - size, value)


def around(offset, size):
    return min(offset, size - offset)


def front_kernel(
    dims,
    cols_hbm, aff_hbm, basis_hbm, deg_hbm, reorder_hbm,
    gram_out, perm_out,
    cols, aff, basis, deg, reorder, halo, halo_deg, ext, iroot, parts,
    gpack, rs_buf, z_src, z_buf, ag_src, ag_buf,
    in_sem, aff_sem, halo_send, halo_recv, rs_send, rs_recv, z_send, z_recv, ag_send, ag_recv, far_sem,
):
    nz, ny, ns, count, block = dims
    plane = ny * ns
    total = plane * nz
    rank = basis.shape[0]
    row, sub = lax.axis_index("rows"), lax.axis_index("sub")
    y, z = row // nz, row % nz
    mine = y * ns + sub
    linear = row * ns + sub

    up, down = wrap(linear + 1, total), wrap(linear + total - 1, total)
    right = (up // ns, up % ns)
    left = (down // ns, down % ns)
    ys = [wrap(y + d, ny) for d in range(ny)]
    subs = [wrap(sub + d, ns) for d in range(ns)]
    plane_offsets = sorted(
        ((dy, ds) for dy in range(ny) for ds in range(ns) if dy or ds),
        key=lambda o: -(2 * around(o[0], ny) + around(o[1], ns)))
    plane_ids = [(ys[dy] * nz + z, subs[ds]) for dy, ds in plane_offsets]
    plane_slots = [ys[dy] * ns + subs[ds] for dy, ds in plane_offsets]
    z_offsets = sorted(range(1, nz), key=lambda d: -around(d, nz))
    z_ids = [(y * nz + wrap(z + d, nz), sub) for d in z_offsets]
    near = nz // 4 if nz >= 8 else nz
    greeted = [device for d, device in zip(z_offsets, z_ids) if around(d, nz) <= near]

    barrier = pltpu.get_barrier_semaphore()

    def signal(device):
        pl.semaphore_signal(barrier, inc=1, device_id=device, device_id_type=MESH)

    def remote(src, dst, send, recv, device):
        return pltpu.make_async_remote_copy(
            src, dst, send, recv, device_id=device, device_id_type=MESH)

    def drain(ref, sem):
        pltpu.make_async_copy(ref, ref, sem).wait()

    signal(left)
    signal(right)

    deg_in = pltpu.make_async_copy(deg_hbm, deg, in_sem.at[0])
    basis_in = pltpu.make_async_copy(basis_hbm, basis, in_sem.at[1])
    cols_in = pltpu.make_async_copy(cols_hbm, cols, in_sem.at[2])
    reorder_in = pltpu.make_async_copy(reorder_hbm, reorder, in_sem.at[3])

    def aff_in(b):
        return pltpu.make_async_copy(aff_hbm.at[b], aff.at[b], aff_sem.at[b])

    inner = tuple(range(REACH, count - REACH))
    outer = tuple(range(REACH)) + tuple(range(count - REACH, count))
    deg_in.start()
    basis_in.start()
    cols_in.start()
    for b in inner:
        aff_in(b).start()
    for device in plane_ids + greeted:
        signal(device)
    for b in outer:
        aff_in(b).start()
    reorder_in.start()

    pl.semaphore_wait(barrier, 2 + len(greeted) + len(plane_ids))

    width = REACH * block
    pieces = deg.shape[0]
    sends = [
        remote(basis_hbm.at[:, pl.ds((count - REACH) * block, width)], halo.at[0],
               halo_send.at[0], halo_recv.at[0], right),
        remote(basis_hbm.at[:, pl.ds(0, width)], halo.at[1],
               halo_send.at[1], halo_recv.at[1], left),
        remote(deg_hbm.at[pieces - 1], halo_deg.at[0], halo_send.at[2], halo_recv.at[2], right),
        remote(deg_hbm.at[0], halo_deg.at[1], halo_send.at[3], halo_recv.at[3], left),
    ]
    for copy in sends:
        copy.start()
    relays = [near, nz - near] if near < nz else []
    for d in relays:
        pl.semaphore_signal(
            far_sem, inc=1, device_id=(y * nz + wrap(z + d, nz), sub), device_id_type=MESH)

    def spread(root, first_row):
        return jnp.concatenate(
            [root[first_row + h : first_row + h + 1, :] for h in range(block // 128)], axis=1)

    def scaled(raw, factor):
        return (raw.astype(F32) * factor).astype(BF16)

    per_block = block // 128
    deg_in.wait()
    for g in range(pieces):
        root = lax.rsqrt(deg[g].astype(F32))
        for j in range(REACH):
            iroot[g * REACH + j] = spread(root, j * per_block)
    basis_in.wait()
    for b in range(count):
        ext[b + REACH] = scaled(basis[:, b * block : (b + 1) * block], iroot[b])
    cols_in.wait()

    first = linear * count

    def picked(k, b, low, high):
        return ext[jnp.clip(cols[k, b] - first + REACH, low, high)]

    def split(b, acc):
        image = acc * iroot[b]
        hi = image.astype(BF16)
        rest = image - hi.astype(F32)
        mid = rest.astype(BF16)
        lo = (rest - mid.astype(F32)).astype(BF16)
        parts[b, :rank, :] = hi
        parts[b, rank:, :] = mid
        return hi, mid, lo

    def gram_of(splits):
        hi, mid, lo = (jnp.concatenate(p, axis=1) for p in zip(*splits))
        g1 = dot_nt(jnp.concatenate([hi, mid, lo], axis=0), hi)
        g2 = dot_nt(jnp.concatenate([hi, mid], axis=0), mid)
        g3 = dot_nt(hi, lo)
        small = g1[2 * rank :] + g2[rank:] + g3
        cross = g1[rank : 2 * rank] + g2[:rank]
        return g1[:rank] + (cross + small)

    for b in inner:
        aff_in(b).wait()
    splits = []
    for b in inner:
        acc = dot_nt(ext[b + REACH], aff[b, 0])
        for k in range(1, 3):
            acc += dot_nt(picked(k, b, REACH, count + REACH - 1), aff[b, k])
        splits.append(split(b, acc))
    gram = gram_of(splits)
    for b in outer:
        aff_in(b).wait()
    starts = [dot_nt(ext[b + REACH], aff[b, 0]) for b in outer]

    for copy in sends:
        copy.wait_recv()
    for side, base in ((0, 0), (1, count + REACH)):
        root = lax.rsqrt(halo_deg[side].astype(F32))
        for j in range(REACH):
            ext[base + j] = scaled(
                halo[side, :, j * block : (j + 1) * block], spread(root, j * per_block))

    splits = []
    for b, acc in zip(outer, starts):
        for k in range(1, 3):
            acc += dot_nt(picked(k, b, 0, count + 2 * REACH - 1), aff[b, k])
        splits.append(split(b, acc))
    gram += gram_of(splits)

    half = rank // 2
    packed = jnp.concatenate([gram[:half], gram[half:]], axis=1)
    per = half // plane
    for q in range(plane):
        gpack[q] = packed[q * per : (q + 1) * per]

    for i, (device, q) in enumerate(zip(plane_ids, plane_slots)):
        remote(gpack.at[q], rs_buf.at[i], rs_send, rs_recv, device).start()

    reorder_in.wait()
    ids = lax.broadcasted_iota(jnp.int32, (block, block), 0)
    for b in range(count):
        pick = jnp.where(ids == reorder[b : b + 1, :], 1.0, 0.0).astype(BF16)
        perm_out[b] = dot(parts[b], pick).astype(BF16)

    drain(rs_buf, rs_recv)
    if relays:
        pl.semaphore_wait(far_sem, len(relays))
    z_src[...] = gpack[mine] + jnp.sum(rs_buf[...], axis=0)
    for i, device in enumerate(z_ids):
        remote(z_src, z_buf.at[i], z_send, z_recv, device).start()
    for copy in sends:
        copy.wait_send()
    drain(rs_buf, rs_send)

    drain(z_buf, z_recv)
    chunk = z_src[...] + jnp.sum(z_buf[...], axis=0)
    ag_src[...] = chunk
    ag_buf[mine] = chunk
    for device in plane_ids:
        remote(ag_src, ag_buf.at[mine], ag_send, ag_recv, device).start()
    drain(z_buf, z_send)
    drain(ag_buf.at[pl.ds(0, plane - 1)], ag_recv)
    for q in range(plane):
        gram_out[q * per : (q + 1) * per] = ag_buf[q]
    drain(ag_buf.at[pl.ds(0, plane - 1)], ag_send)


def back_kernel(scale, gram_ref, perm, out_hbm, out, out_sem):
    count, depth, block = perm.shape
    rank = depth // 2
    half = rank // 2
    tiles = rank // 8

    packed = gram_ref[...]
    low = pltpu.roll(packed, rank, 1)
    lane = lax.broadcasted_iota(jnp.int32, (8, 2 * rank), 1)
    sublane = lax.broadcasted_iota(jnp.int32, (8, 2 * rank), 0)
    state = []
    for t in range(tiles):
        source = low if t < tiles // 2 else packed
        r = (8 * t) % half
        eye = jnp.where(lane == sublane + 8 * t, 1.0, 0.0)
        state.append(jnp.where(lane < rank, eye, source[r : r + 8]))

    def row(v, j):
        return jnp.broadcast_to(v[j : j + 1, :], v.shape)

    rows = []
    for t in range(tiles):
        cols = []
        for j in range(8):
            k = rank + 8 * t + j
            cols.append([jnp.broadcast_to(state[v][:, k : k + 1], (8, 2 * rank)) for v in range(t, tiles)])
        pivots = None
        mults = []
        pivot_rows = []
        for j in range(8):
            pivot = row(cols[j][0], j)
            pivots = pivot if pivots is None else jnp.where(sublane == j, pivot, pivots)
            inv = 1.0 / pivot
            mult = [c * inv for c in cols[j]]
            mult[0] = jnp.where(sublane > j, mult[0], 0.0)
            for jj in range(j + 1, 8):
                top = row(cols[jj][0], j)
                cols[jj] = [c - m * top for c, m in zip(cols[jj], mult)]
            pivot_row = row(state[t], j)
            state[t] = state[t] - mult[0] * pivot_row
            mults.append(mult)
            pivot_rows.append(pivot_row)
        for v in range(t + 1, tiles):
            upd = mults[0][v - t] * pivot_rows[0]
            for j in range(1, 8):
                upd = upd + mults[j][v - t] * pivot_rows[j]
            state[v] = state[v] - upd
        rows.append(state[t] * (lax.rsqrt(pivots) * scale))

    inverse = jnp.concatenate(rows, axis=0)[:, :rank]
    hi = inverse.astype(BF16)
    mid = (inverse - hi.astype(F32)).astype(BF16)
    left = jnp.concatenate(
        [jnp.concatenate([hi, hi], axis=1), jnp.concatenate([mid, mid], axis=1)], axis=0)

    def out_copy(b):
        cols = pl.ds(b * block, block)
        return pltpu.make_async_copy(out.at[:, cols], out_hbm.at[:, cols], out_sem.at[b])

    for b in range(count):
        both = dot(left, perm[b])
        out[:, b * block : (b + 1) * block] = both[:rank] + both[rank:]
        out_copy(b).start()
    for b in range(count):
        out_copy(b).wait()


def body(ny, nz, ns, affinity, old_basis, degrees, column_blocks, reorder):
    count, _, block, _ = affinity.shape
    rows_here, rank = old_basis.shape
    plane = ny * ns
    per = rank // 2 // plane
    anywhere = pl.BlockSpec(memory_space=pl.ANY)
    vmem = pl.BlockSpec(memory_space=pltpu.VMEM)
    dma = pltpu.SemaphoreType.DMA
    width = REACH * block // 128
    gram, perm = pl.pallas_call(
        functools.partial(front_kernel, (nz, ny, ns, count, block)),
        name="front",
        out_shape=(
            pltpu.VMEM((rank // 2, 2 * rank), F32),
            pltpu.VMEM((count, 2 * rank, block), BF16),
        ),
        in_specs=[anywhere] * 5,
        out_specs=(vmem, vmem),
        scratch_shapes=[
            pltpu.SMEM(column_blocks.shape[::-1], jnp.int32),
            pltpu.VMEM(affinity.shape, BF16),
            pltpu.VMEM((rank, rows_here), BF16),
            pltpu.VMEM((count // REACH, width, 128), jnp.int32),
            pltpu.VMEM(reorder.shape, jnp.int32),
            pltpu.VMEM((2, rank, REACH * block), BF16),
            pltpu.VMEM((2, width, 128), jnp.int32),
            pltpu.VMEM((count + 2 * REACH, rank, block), BF16),
            pltpu.VMEM((count, 1, block), F32),
            pltpu.VMEM((count, 2 * rank, block), BF16),
            pltpu.VMEM((plane, per, 2 * rank), F32),
            pltpu.VMEM((plane - 1, per, 2 * rank), F32),
            pltpu.VMEM((per, 2 * rank), F32),
            pltpu.VMEM((nz - 1, per, 2 * rank), F32),
            pltpu.VMEM((per, 2 * rank), F32),
            pltpu.VMEM((plane, per, 2 * rank), F32),
            dma((4,)), dma((count,)), dma((4,)), dma((4,)),
            dma, dma, dma, dma, dma, dma, pltpu.SemaphoreType.REGULAR,
        ],
        compiler_params=pltpu.CompilerParams(collective_id=0, has_side_effects=True),
    )(column_blocks.T, affinity, old_basis.T, degrees.reshape(-1, width, 128), reorder)
    items = rows_here * lax.axis_size("rows") * lax.axis_size("sub")
    out = pl.pallas_call(
        functools.partial(back_kernel, math.sqrt(items)),
        name="back",
        out_shape=jax.ShapeDtypeStruct((rank, rows_here), F32),
        in_specs=[vmem, vmem],
        out_specs=anywhere,
        scratch_shapes=[pltpu.VMEM((rank, rows_here), F32), dma((count,))],
    )(*(pltpu.with_memory_space_constraint(a, pltpu.VMEM) for a in (gram, perm)))
    return out.T


def solution(mesh):
    rows, ns = mesh.shape["rows"], mesh.shape["sub"]
    nz = min(16, rows)
    both = P(("rows", "sub"))
    return jax.shard_map(
        functools.partial(body, rows // nz, nz, ns),
        mesh=mesh, in_specs=(both,) * 5, out_specs=both, check_vma=False,
    )
```

```python
import functools
import math

import jax
import jax.numpy as jnp
from jax import lax
from jax.experimental import pallas as pl
from jax.experimental.pallas import tpu as pltpu
from jax.sharding import PartitionSpec as P

MESH = pl.DeviceIdType.MESH
REACH = 2
DEPTHS = (2, 2, 2, 2)
NT = (((1,), (1,)), ((), ()))
F32 = jnp.float32
BF16 = jnp.bfloat16


def dot(a, b):
    return jnp.dot(a, b, preferred_element_type=F32)


def dot_nt(a, b):
    return lax.dot_general(a, b, NT, preferred_element_type=F32)


def wrap(value, size):
    return jnp.where(value >= size, value - size, value)


def around(offset, size):
    return min(offset, size - offset)


def tree_sum(terms):
    while len(terms) > 1:
        terms = [sum(terms[i : i + 2][1:], terms[i]) for i in range(0, len(terms), 2)]
    return terms[0]


def front_kernel(
    dims,
    cols_hbm, aff_hbm, basis_hbm, deg_hbm, reorder_hbm,
    gram_out, perm_out,
    cols, aff, basis, deg, reorder, halo, halo_deg, ext, iroot, parts,
    gpack, rs_buf, z_src, z_buf, ag_src, ag_buf,
    in_sem, aff_sem, halo_send, halo_recv, rs_send, rs_recv, z_send, z_recv, ag_send, ag_recv, plane_sem, far_sem,
):
    nz, ny, ns, count, block = dims
    plane = ny * ns
    total = plane * nz
    rank = basis.shape[0]
    row, sub = lax.axis_index("rows"), lax.axis_index("sub")
    y, z = row // nz, row % nz
    mine = y * ns + sub
    linear = row * ns + sub

    up, down = wrap(linear + 1, total), wrap(linear + total - 1, total)
    right = (up // ns, up % ns)
    left = (down // ns, down % ns)
    ys = [wrap(y + d, ny) for d in range(ny)]
    subs = [wrap(sub + d, ns) for d in range(ns)]
    plane_offsets = sorted(
        ((dy, ds) for dy in range(ny) for ds in range(ns) if dy or ds),
        key=lambda o: -(2 * around(o[0], ny) + around(o[1], ns)))
    plane_ids = [(ys[dy] * nz + z, subs[ds]) for dy, ds in plane_offsets]
    plane_slots = [ys[dy] * ns + subs[ds] for dy, ds in plane_offsets]
    z_offsets = sorted(range(1, nz), key=lambda d: -around(d, nz))
    z_ids = [(y * nz + wrap(z + d, nz), sub) for d in z_offsets]
    y_line = [(ys[d] * nz + z, sub) for d in range(1, ny)]
    x_line = [(row, subs[d]) for d in range(1, ns)]

    def z_id(d):
        return (y * nz + wrap(z + d, nz), sub)

    near = max(1, nz // 8)
    steps = [near, 2 * near]
    z_line = [z_id(d) for d in range(1, nz) if around(d, nz) <= near]

    barrier = pltpu.get_barrier_semaphore()

    def signal(device):
        pl.semaphore_signal(barrier, inc=1, device_id=device, device_id_type=MESH)

    def remote(src, dst, send, recv, device):
        return pltpu.make_async_remote_copy(
            src, dst, send, recv, device_id=device, device_id_type=MESH)

    def drain(ref, sem):
        pltpu.make_async_copy(ref, ref, sem).wait()

    signal(left)
    signal(right)

    deg_in = pltpu.make_async_copy(deg_hbm, deg, in_sem.at[0])
    basis_in = pltpu.make_async_copy(basis_hbm, basis, in_sem.at[1])
    cols_in = pltpu.make_async_copy(cols_hbm, cols, in_sem.at[2])
    reorder_in = pltpu.make_async_copy(reorder_hbm, reorder, in_sem.at[3])

    def aff_in(b):
        return pltpu.make_async_copy(aff_hbm.at[b], aff.at[b], aff_sem.at[b])

    inner = tuple(range(REACH, count - REACH))
    outer = tuple(range(REACH)) + tuple(range(count - REACH, count))
    deg_in.start()
    basis_in.start()
    cols_in.start()
    for b in inner:
        aff_in(b).start()
    for device in x_line + y_line + z_line:
        signal(device)
    for b in outer:
        aff_in(b).start()
    reorder_in.start()

    pl.semaphore_wait(barrier, 2 + len(x_line) + len(y_line) + len(z_line))

    width = REACH * block
    pieces = deg.shape[0]
    sends = [
        remote(basis.at[:, pl.ds((count - REACH) * block, width)], halo.at[0],
               halo_send.at[0], halo_recv.at[0], right),
        remote(basis.at[:, pl.ds(0, width)], halo.at[1],
               halo_send.at[1], halo_recv.at[1], left),
        remote(deg_hbm.at[pieces - 1], halo_deg.at[0], halo_send.at[2], halo_recv.at[2], right),
        remote(deg_hbm.at[0], halo_deg.at[1], halo_send.at[3], halo_recv.at[3], left),
    ]
    basis_in.wait()
    for copy in sends:
        copy.start()

    def tell(sem, devices):
        for device in devices:
            pl.semaphore_signal(sem, inc=1, device_id=device, device_id_type=MESH)

    tell(plane_sem, y_line)
    tell(far_sem.at[0], [z_id(steps[0]), z_id(nz - steps[0])])

    def spread(root, first_row):
        return jnp.concatenate(
            [root[first_row + h : first_row + h + 1, :] for h in range(block // 128)], axis=1)

    def scaled(raw, factor):
        return (raw.astype(F32) * factor).astype(BF16)

    per_block = block // 128
    deg_in.wait()
    for g in range(pieces):
        root = lax.rsqrt(deg[g].astype(F32))
        for j in range(REACH):
            iroot[g * REACH + j] = spread(root, j * per_block)
    for b in range(count):
        ext[b + REACH] = scaled(basis[:, b * block : (b + 1) * block], iroot[b])
    cols_in.wait()

    first = linear * count

    def picked(k, b, low, high):
        return ext[jnp.clip(cols[k, b] - first + REACH, low, high)]

    def split(b, acc):
        image = acc * iroot[b]
        hi = image.astype(BF16)
        rest = image - hi.astype(F32)
        mid = rest.astype(BF16)
        lo = (rest - mid.astype(F32)).astype(BF16)
        parts[b, :rank, :] = hi
        parts[b, rank:, :] = mid
        return hi, mid, lo

    def gram_of(splits):
        hi, mid, lo = (jnp.concatenate(p, axis=1) for p in zip(*splits))
        g1 = dot_nt(jnp.concatenate([hi, mid, lo], axis=0), hi)
        g2 = dot_nt(jnp.concatenate([hi, mid], axis=0), mid)
        g3 = dot_nt(hi, lo)
        small = g1[2 * rank :] + g2[rank:] + g3
        cross = g1[rank : 2 * rank] + g2[:rank]
        return g1[:rank] + (cross + small)

    for b in inner:
        aff_in(b).wait()
    splits = []
    for b in inner:
        acc = dot_nt(ext[b + REACH], aff[b, 0])
        for k in range(1, 3):
            acc += dot_nt(picked(k, b, REACH, count + REACH - 1), aff[b, k])
        splits.append(split(b, acc))
    gram = gram_of(splits)
    for b in outer:
        aff_in(b).wait()
    starts = [dot_nt(ext[b + REACH], aff[b, 0]) for b in outer]

    pl.semaphore_wait(far_sem.at[0], 2)
    tell(far_sem.at[1], [z_id(steps[1]), z_id(nz - steps[1])])
    for copy in sends:
        copy.wait_recv()
    for side, base in ((0, 0), (1, count + REACH)):
        root = lax.rsqrt(halo_deg[side].astype(F32))
        for j in range(REACH):
            ext[base + j] = scaled(
                halo[side, :, j * block : (j + 1) * block], spread(root, j * per_block))

    splits = []
    for b, acc in zip(outer, starts):
        for k in range(1, 3):
            acc += dot_nt(picked(k, b, 0, count + 2 * REACH - 1), aff[b, k])
        splits.append(split(b, acc))
    gram += gram_of(splits)

    half = rank // 2
    packed = jnp.concatenate([gram[:half], gram[half:]], axis=1)
    per = half // plane
    for q in range(plane):
        gpack[q] = packed[q * per : (q + 1) * per]

    if y_line:
        pl.semaphore_wait(plane_sem, len(y_line))
    for i, (device, q) in enumerate(zip(plane_ids, plane_slots)):
        remote(gpack.at[q], rs_buf.at[i], rs_send, rs_recv, device).start()

    reorder_in.wait()
    ids = lax.broadcasted_iota(jnp.int32, (block, block), 0)
    for b in range(count):
        pick = jnp.where(ids == reorder[b : b + 1, :], 1.0, 0.0).astype(BF16)
        perm_out[b] = dot(parts[b], pick).astype(BF16)

    drain(rs_buf, rs_recv)
    pl.semaphore_wait(far_sem.at[1], 2)
    z_src[...] = tree_sum([gpack[mine]] + [rs_buf[i] for i in range(plane - 1)])
    for i, device in enumerate(z_ids):
        remote(z_src, z_buf.at[i], z_send, z_recv, device).start()
    for copy in sends:
        copy.wait_send()
    drain(rs_buf, rs_send)

    drain(z_buf, z_recv)
    chunk = tree_sum([z_src[...]] + [z_buf[i] for i in range(nz - 1)])
    ag_src[...] = chunk
    ag_buf[mine] = chunk
    for device in plane_ids:
        remote(ag_src, ag_buf.at[mine], ag_send, ag_recv, device).start()
    drain(z_buf, z_send)
    drain(ag_buf.at[pl.ds(0, plane - 1)], ag_recv)
    for q in range(plane):
        gram_out[q * per : (q + 1) * per] = ag_buf[q]
    drain(ag_buf.at[pl.ds(0, plane - 1)], ag_send)


def back_kernel(scale, gram_ref, perm, out_hbm, out, out_sem):
    count, depth, block = perm.shape
    rank = depth // 2
    half = rank // 2
    tiles = rank // 8

    packed = gram_ref[...]
    low = pltpu.roll(packed, rank, 1)
    lane = lax.broadcasted_iota(jnp.int32, (8, 2 * rank), 1)
    sublane = lax.broadcasted_iota(jnp.int32, (8, 2 * rank), 0)
    state = []
    for t in range(tiles):
        source = low if t < tiles // 2 else packed
        r = (8 * t) % half
        eye = jnp.where(lane == sublane + 8 * t, 1.0, 0.0)
        state.append(jnp.where(lane < rank, eye, source[r : r + 8]))

    def row(v, j):
        return jnp.broadcast_to(v[j : j + 1, :], v.shape)

    rows = []
    start = 0
    for depth in DEPTHS:
        span = range(start, tiles)
        cols = []
        for j in range(8 * depth):
            k = rank + 8 * start + j
            cols.append({v: jnp.broadcast_to(state[v][:, k : k + 1], (8, 2 * rank))
                         for v in span if v >= start + j // 8})
        mults = []
        pivot_rows = []
        pivots = [None] * depth
        for j in range(8 * depth):
            t, i = start + j // 8, j % 8
            pivot = row(cols[j][t], i)
            d = j // 8
            pivots[d] = pivot if i == 0 else jnp.where(sublane == i, pivot, pivots[d])
            inv = 1.0 / pivot
            mult = {v: c * inv for v, c in cols[j].items()}
            for jj in range(j + 1, 8 * depth):
                top = row(cols[j][start + jj // 8], jj % 8)
                cols[jj] = {v: c - mult[v] * top for v, c in cols[jj].items()}
            mult[t] = jnp.where(sublane > i, mult[t], 0.0)
            pivot_row = row(state[t], i)
            for v in range(t, start + depth):
                state[v] = state[v] - mult[v] * pivot_row
            mults.append(mult)
            pivot_rows.append(pivot_row)
        for v in range(start + depth, tiles):
            for mult, pivot_row in zip(mults, pivot_rows):
                state[v] = state[v] - mult[v] * pivot_row
        for d in range(depth):
            rows.append(state[start + d] * (lax.rsqrt(pivots[d]) * scale))
        start += depth

    inverse = jnp.concatenate(rows, axis=0)[:, :rank]
    hi = inverse.astype(BF16)
    mid = (inverse - hi.astype(F32)).astype(BF16)
    left = jnp.concatenate(
        [jnp.concatenate([hi, hi], axis=1), jnp.concatenate([mid, mid], axis=1)], axis=0)

    def out_copy(b):
        cols = pl.ds(b * block, block)
        return pltpu.make_async_copy(out.at[:, cols], out_hbm.at[:, cols], out_sem.at[b])

    for b in range(count):
        both = dot(left, perm[b])
        out[:, b * block : (b + 1) * block] = both[:rank] + both[rank:]
        out_copy(b).start()
    for b in range(count):
        out_copy(b).wait()


def body(ny, nz, ns, affinity, old_basis, degrees, column_blocks, reorder):
    count, _, block, _ = affinity.shape
    rows_here, rank = old_basis.shape
    plane = ny * ns
    per = rank // 2 // plane
    anywhere = pl.BlockSpec(memory_space=pl.ANY)
    vmem = pl.BlockSpec(memory_space=pltpu.VMEM)
    dma = pltpu.SemaphoreType.DMA
    width = REACH * block // 128
    gram, perm = pl.pallas_call(
        functools.partial(front_kernel, (nz, ny, ns, count, block)),
        name="front",
        out_shape=(
            pltpu.VMEM((rank // 2, 2 * rank), F32),
            pltpu.VMEM((count, 2 * rank, block), BF16),
        ),
        in_specs=[anywhere] * 5,
        out_specs=(vmem, vmem),
        scratch_shapes=[
            pltpu.SMEM(column_blocks.shape[::-1], jnp.int32),
            pltpu.VMEM(affinity.shape, BF16),
            pltpu.VMEM((rank, rows_here), BF16),
            pltpu.VMEM((count // REACH, width, 128), jnp.int32),
            pltpu.VMEM(reorder.shape, jnp.int32),
            pltpu.VMEM((2, rank, REACH * block), BF16),
            pltpu.VMEM((2, width, 128), jnp.int32),
            pltpu.VMEM((count + 2 * REACH, rank, block), BF16),
            pltpu.VMEM((count, 1, block), F32),
            pltpu.VMEM((count, 2 * rank, block), BF16),
            pltpu.VMEM((plane, per, 2 * rank), F32),
            pltpu.VMEM((plane - 1, per, 2 * rank), F32),
            pltpu.VMEM((per, 2 * rank), F32),
            pltpu.VMEM((nz - 1, per, 2 * rank), F32),
            pltpu.VMEM((per, 2 * rank), F32),
            pltpu.VMEM((plane, per, 2 * rank), F32),
            dma((4,)), dma((count,)), dma((4,)), dma((4,)),
            dma, dma, dma, dma, dma, dma,
            pltpu.SemaphoreType.REGULAR, pltpu.SemaphoreType.REGULAR((2,)),
        ],
        compiler_params=pltpu.CompilerParams(collective_id=0, has_side_effects=True),
    )(column_blocks.T, affinity, old_basis.T, degrees.reshape(-1, width, 128), reorder)
    items = rows_here * lax.axis_size("rows") * lax.axis_size("sub")
    out = pl.pallas_call(
        functools.partial(back_kernel, math.sqrt(items)),
        name="back",
        out_shape=jax.ShapeDtypeStruct((rank, rows_here), F32),
        in_specs=[vmem, vmem],
        out_specs=anywhere,
        scratch_shapes=[pltpu.VMEM((rank, rows_here), F32), dma((count,))],
    )(*(pltpu.with_memory_space_constraint(a, pltpu.VMEM) for a in (gram, perm)))
    return out.T


def solution(mesh):
    rows, ns = mesh.shape["rows"], mesh.shape["sub"]
    nz = min(16, rows)
    both = P(("rows", "sub"))
    return jax.shard_map(
        functools.partial(body, rows // nz, nz, ns),
        mesh=mesh, in_specs=(both,) * 5, out_specs=both, check_vma=False,
    )
```

```python
import functools
import math

import jax
import jax.numpy as jnp
from jax import lax
from jax.experimental import pallas as pl
from jax.experimental.pallas import tpu as pltpu
from jax.sharding import PartitionSpec as P

MESH = pl.DeviceIdType.MESH
REACH = 2
NY = 4
DEPTHS = (2, 2, 2, 2)
NT = (((1,), (1,)), ((), ()))
F32 = jnp.float32
BF16 = jnp.bfloat16


def dot(a, b):
    return jnp.dot(a, b, preferred_element_type=F32)


def dot_nt(a, b):
    return lax.dot_general(a, b, NT, preferred_element_type=F32)


def wrap(value, size):
    return jnp.where(value >= size, value - size, value)


def around(offset, size):
    return min(offset, size - offset)


def tree_sum(terms):
    while len(terms) > 1:
        terms = [sum(terms[i : i + 2][1:], terms[i]) for i in range(0, len(terms), 2)]
    return terms[0]


def front_kernel(
    dims,
    cols_hbm, aff_hbm, basis_hbm, deg_hbm, reorder_hbm,
    gram_out, perm_out,
    cols, aff, basis, deg, reorder, halo, halo_deg, ext, iroot, parts,
    gpack, core_buf, gsum, rs_buf, z_src, z_buf, ag_src, ag_buf,
    in_sem, aff_sem, halo_send, halo_recv, core_send, core_recv, rs_send, rs_recv, z_send, z_recv, ag_send, ag_recv, plane_sem, far_sem,
):
    nz, ny, ns, count, block = dims
    nx = ns // 2
    plane = ny * nx
    total = ny * nz * ns
    rank = basis.shape[0]
    row, sub = lax.axis_index("rows"), lax.axis_index("sub")
    y, z = row // nz, row % nz
    x, core = sub // 2, sub % 2
    mine = y * nx + x
    linear = row * ns + sub

    up, down = wrap(linear + 1, total), wrap(linear + total - 1, total)
    right = (up // ns, up % ns)
    left = (down // ns, down % ns)
    ys = [wrap(y + d, ny) for d in range(ny)]
    xs = [wrap(x + d, nx) for d in range(nx)]
    plane_offsets = sorted(
        ((dy, dx) for dy in range(ny) for dx in range(nx) if dy or dx),
        key=lambda o: -(around(o[0], ny) + around(o[1], nx)))
    plane_ids = [(ys[dy] * nz + z, 2 * xs[dx] + core) for dy, dx in plane_offsets]
    plane_slots = [ys[dy] * nx + xs[dx] for dy, dx in plane_offsets]
    partner = (row, sub + 1 - 2 * core)
    z_offsets = sorted(range(1, nz), key=lambda d: -around(d, nz))
    z_ids = [(y * nz + wrap(z + d, nz), sub) for d in z_offsets]
    y_line = [(ys[d] * nz + z, sub) for d in range(1, ny)]
    x_line = [(row, 2 * xs[d] + core) for d in range(1, nx)]

    def z_id(d):
        return (y * nz + wrap(z + d, nz), sub)

    near = max(1, nz // 8)
    steps = [near, 2 * near]
    z_line = [z_id(d) for d in range(1, nz) if around(d, nz) <= near]

    barrier = pltpu.get_barrier_semaphore()

    def signal(device):
        pl.semaphore_signal(barrier, inc=1, device_id=device, device_id_type=MESH)

    def remote(src, dst, send, recv, device):
        return pltpu.make_async_remote_copy(
            src, dst, send, recv, device_id=device, device_id_type=MESH)

    def drain(ref, sem):
        pltpu.make_async_copy(ref, ref, sem).wait()

    signal(left)
    signal(right)

    deg_in = pltpu.make_async_copy(deg_hbm, deg, in_sem.at[0])
    basis_in = pltpu.make_async_copy(basis_hbm, basis, in_sem.at[1])
    cols_in = pltpu.make_async_copy(cols_hbm, cols, in_sem.at[2])
    reorder_in = pltpu.make_async_copy(reorder_hbm, reorder, in_sem.at[3])

    def aff_in(b):
        return pltpu.make_async_copy(aff_hbm.at[b], aff.at[b], aff_sem.at[b])

    inner = tuple(range(REACH, count - REACH))
    outer = tuple(range(REACH)) + tuple(range(count - REACH, count))
    deg_in.start()
    basis_in.start()
    cols_in.start()
    for b in inner:
        aff_in(b).start()
    for device in [partner] + x_line + y_line + z_line:
        signal(device)
    for b in outer:
        aff_in(b).start()
    reorder_in.start()

    pl.semaphore_wait(barrier, 3 + len(x_line) + len(y_line) + len(z_line))

    width = REACH * block
    pieces = deg.shape[0]
    sends = [
        remote(basis.at[:, pl.ds((count - REACH) * block, width)], halo.at[0],
               halo_send.at[0], halo_recv.at[0], right),
        remote(basis.at[:, pl.ds(0, width)], halo.at[1],
               halo_send.at[1], halo_recv.at[1], left),
        remote(deg_hbm.at[pieces - 1], halo_deg.at[0], halo_send.at[2], halo_recv.at[2], right),
        remote(deg_hbm.at[0], halo_deg.at[1], halo_send.at[3], halo_recv.at[3], left),
    ]
    basis_in.wait()
    for copy in sends:
        copy.start()

    def tell(sem, devices):
        for device in devices:
            pl.semaphore_signal(sem, inc=1, device_id=device, device_id_type=MESH)

    tell(plane_sem, y_line)
    tell(far_sem.at[0], [z_id(steps[0]), z_id(nz - steps[0])])

    def spread(root, first_row):
        return jnp.concatenate(
            [root[first_row + h : first_row + h + 1, :] for h in range(block // 128)], axis=1)

    def scaled(raw, factor):
        return (raw.astype(F32) * factor).astype(BF16)

    per_block = block // 128
    deg_in.wait()
    for g in range(pieces):
        root = lax.rsqrt(deg[g].astype(F32))
        for j in range(REACH):
            iroot[g * REACH + j] = spread(root, j * per_block)
    for b in range(count):
        ext[b + REACH] = scaled(basis[:, b * block : (b + 1) * block], iroot[b])
    cols_in.wait()

    first = linear * count

    def picked(k, b, low, high):
        return ext[jnp.clip(cols[k, b] - first + REACH, low, high)]

    def split(b, acc):
        image = acc * iroot[b]
        hi = image.astype(BF16)
        rest = image - hi.astype(F32)
        mid = rest.astype(BF16)
        lo = (rest - mid.astype(F32)).astype(BF16)
        parts[b, :rank, :] = hi
        parts[b, rank:, :] = mid
        return hi, mid, lo

    def gram_of(splits):
        hi, mid, lo = (jnp.concatenate(p, axis=1) for p in zip(*splits))
        g1 = dot_nt(jnp.concatenate([hi, mid, lo], axis=0), hi)
        g2 = dot_nt(jnp.concatenate([hi, mid], axis=0), mid)
        g3 = dot_nt(hi, lo)
        small = g1[2 * rank :] + g2[rank:] + g3
        cross = g1[rank : 2 * rank] + g2[:rank]
        return g1[:rank] + (cross + small)

    for b in inner:
        aff_in(b).wait()
    splits = []
    for b in inner:
        acc = dot_nt(ext[b + REACH], aff[b, 0])
        for k in range(1, 3):
            acc += dot_nt(picked(k, b, REACH, count + REACH - 1), aff[b, k])
        splits.append(split(b, acc))
    gram = gram_of(splits)
    for b in outer:
        aff_in(b).wait()
    starts = [dot_nt(ext[b + REACH], aff[b, 0]) for b in outer]

    pl.semaphore_wait(far_sem.at[0], 2)
    tell(far_sem.at[1], [z_id(steps[1]), z_id(nz - steps[1])])
    for copy in sends:
        copy.wait_recv()
    for side, base in ((0, 0), (1, count + REACH)):
        root = lax.rsqrt(halo_deg[side].astype(F32))
        for j in range(REACH):
            ext[base + j] = scaled(
                halo[side, :, j * block : (j + 1) * block], spread(root, j * per_block))

    splits = []
    for b, acc in zip(outer, starts):
        for k in range(1, 3):
            acc += dot_nt(picked(k, b, 0, count + 2 * REACH - 1), aff[b, k])
        splits.append(split(b, acc))
    gram += gram_of(splits)

    half = rank // 2
    packed = jnp.concatenate([gram[:half], gram[half:]], axis=1)
    per = half // plane
    for q in range(plane):
        gpack[q] = packed[q * per : (q + 1) * per]
    swap = remote(gpack, core_buf, core_send, core_recv, partner)
    swap.start()
    swap.wait_recv()
    gsum[...] = gpack[...] + core_buf[...]

    if y_line:
        pl.semaphore_wait(plane_sem, len(y_line))
    for i, (device, q) in enumerate(zip(plane_ids, plane_slots)):
        remote(gsum.at[q], rs_buf.at[i], rs_send, rs_recv, device).start()

    reorder_in.wait()
    ids = lax.broadcasted_iota(jnp.int32, (block, block), 0)
    for b in range(count):
        pick = jnp.where(ids == reorder[b : b + 1, :], 1.0, 0.0).astype(BF16)
        perm_out[b] = dot(parts[b], pick).astype(BF16)

    drain(rs_buf, rs_recv)
    pl.semaphore_wait(far_sem.at[1], 2)
    z_src[...] = tree_sum([gsum[mine]] + [rs_buf[i] for i in range(plane - 1)])
    for i, device in enumerate(z_ids):
        remote(z_src, z_buf.at[i], z_send, z_recv, device).start()
    for copy in sends:
        copy.wait_send()
    swap.wait_send()
    drain(rs_buf, rs_send)

    drain(z_buf, z_recv)
    chunk = tree_sum([z_src[...]] + [z_buf[i] for i in range(nz - 1)])
    ag_src[...] = chunk
    ag_buf[mine] = chunk
    for device in plane_ids:
        remote(ag_src, ag_buf.at[mine], ag_send, ag_recv, device).start()
    drain(z_buf, z_send)
    drain(ag_buf.at[pl.ds(0, plane - 1)], ag_recv)
    for q in range(plane):
        gram_out[q * per : (q + 1) * per] = ag_buf[q]
    drain(ag_buf.at[pl.ds(0, plane - 1)], ag_send)


def back_kernel(scale, gram_ref, perm, out_hbm, out, out_sem):
    count, depth, block = perm.shape
    rank = depth // 2
    half = rank // 2
    tiles = rank // 8

    packed = gram_ref[...]
    low = pltpu.roll(packed, rank, 1)
    lane = lax.broadcasted_iota(jnp.int32, (8, 2 * rank), 1)
    sublane = lax.broadcasted_iota(jnp.int32, (8, 2 * rank), 0)
    state = []
    for t in range(tiles):
        source = low if t < tiles // 2 else packed
        r = (8 * t) % half
        eye = jnp.where(lane == sublane + 8 * t, 1.0, 0.0)
        state.append(jnp.where(lane < rank, eye, source[r : r + 8]))

    def row(v, j):
        return jnp.broadcast_to(v[j : j + 1, :], v.shape)

    rows = []
    start = 0
    for depth in DEPTHS:
        span = range(start, tiles)
        cols = []
        for j in range(8 * depth):
            k = rank + 8 * start + j
            cols.append({v: jnp.broadcast_to(state[v][:, k : k + 1], (8, 2 * rank))
                         for v in span if v >= start + j // 8})
        mults = []
        pivot_rows = []
        pivots = [None] * depth
        for j in range(8 * depth):
            t, i = start + j // 8, j % 8
            pivot = row(cols[j][t], i)
            d = j // 8
            pivots[d] = pivot if i == 0 else jnp.where(sublane == i, pivot, pivots[d])
            inv = 1.0 / pivot
            mult = {v: c * inv for v, c in cols[j].items()}
            for jj in range(j + 1, 8 * depth):
                top = row(cols[j][start + jj // 8], jj % 8)
                cols[jj] = {v: c - mult[v] * top for v, c in cols[jj].items()}
            mult[t] = jnp.where(sublane > i, mult[t], 0.0)
            pivot_row = row(state[t], i)
            for v in range(t, start + depth):
                state[v] = state[v] - mult[v] * pivot_row
            mults.append(mult)
            pivot_rows.append(pivot_row)
        for v in range(start + depth, tiles):
            for mult, pivot_row in zip(mults, pivot_rows):
                state[v] = state[v] - mult[v] * pivot_row
        for d in range(depth):
            rows.append(state[start + d] * (lax.rsqrt(pivots[d]) * scale))
        start += depth

    inverse = jnp.concatenate(rows, axis=0)[:, :rank]
    hi = inverse.astype(BF16)
    mid = (inverse - hi.astype(F32)).astype(BF16)
    left = jnp.concatenate(
        [jnp.concatenate([hi, hi], axis=1), jnp.concatenate([mid, mid], axis=1)], axis=0)

    def out_copy(b):
        cols = pl.ds(b * block, block)
        return pltpu.make_async_copy(out.at[:, cols], out_hbm.at[:, cols], out_sem.at[b])

    for b in range(count):
        both = dot(left, perm[b])
        out[:, b * block : (b + 1) * block] = both[:rank] + both[rank:]
        out_copy(b).start()
    for b in range(count):
        out_copy(b).wait()


def body(ny, nz, ns, affinity, old_basis, degrees, column_blocks, reorder):
    count, _, block, _ = affinity.shape
    rows_here, rank = old_basis.shape
    plane = ny * (ns // 2)
    per = rank // 2 // plane
    anywhere = pl.BlockSpec(memory_space=pl.ANY)
    vmem = pl.BlockSpec(memory_space=pltpu.VMEM)
    dma = pltpu.SemaphoreType.DMA
    width = REACH * block // 128
    gram, perm = pl.pallas_call(
        functools.partial(front_kernel, (nz, ny, ns, count, block)),
        name="front",
        out_shape=(
            pltpu.VMEM((rank // 2, 2 * rank), F32),
            pltpu.VMEM((count, 2 * rank, block), BF16),
        ),
        in_specs=[anywhere] * 5,
        out_specs=(vmem, vmem),
        scratch_shapes=[
            pltpu.SMEM(column_blocks.shape[::-1], jnp.int32),
            pltpu.VMEM(affinity.shape, BF16),
            pltpu.VMEM((rank, rows_here), BF16),
            pltpu.VMEM((count // REACH, width, 128), jnp.int32),
            pltpu.VMEM(reorder.shape, jnp.int32),
            pltpu.VMEM((2, rank, REACH * block), BF16),
            pltpu.VMEM((2, width, 128), jnp.int32),
            pltpu.VMEM((count + 2 * REACH, rank, block), BF16),
            pltpu.VMEM((count, 1, block), F32),
            pltpu.VMEM((count, 2 * rank, block), BF16),
            pltpu.VMEM((plane, per, 2 * rank), F32),
            pltpu.VMEM((plane, per, 2 * rank), F32),
            pltpu.VMEM((plane, per, 2 * rank), F32),
            pltpu.VMEM((plane - 1, per, 2 * rank), F32),
            pltpu.VMEM((per, 2 * rank), F32),
            pltpu.VMEM((nz - 1, per, 2 * rank), F32),
            pltpu.VMEM((per, 2 * rank), F32),
            pltpu.VMEM((plane, per, 2 * rank), F32),
            dma((4,)), dma((count,)), dma((4,)), dma((4,)),
            dma, dma, dma, dma, dma, dma, dma, dma,
            pltpu.SemaphoreType.REGULAR, pltpu.SemaphoreType.REGULAR((2,)),
        ],
        compiler_params=pltpu.CompilerParams(collective_id=0, has_side_effects=True),
    )(column_blocks.T, affinity, old_basis.T, degrees.reshape(-1, width, 128), reorder)
    items = rows_here * lax.axis_size("rows") * lax.axis_size("sub")
    out = pl.pallas_call(
        functools.partial(back_kernel, math.sqrt(items)),
        name="back",
        out_shape=jax.ShapeDtypeStruct((rank, rows_here), F32),
        in_specs=[vmem, vmem],
        out_specs=anywhere,
        scratch_shapes=[pltpu.VMEM((rank, rows_here), F32), dma((count,))],
    )(*(pltpu.with_memory_space_constraint(a, pltpu.VMEM) for a in (gram, perm)))
    return out.T


def solution(mesh):
    rows, ns = mesh.shape["rows"], mesh.shape["sub"]
    nz = rows // NY
    both = P(("rows", "sub"))
    return jax.shard_map(
        functools.partial(body, rows // nz, nz, ns),
        mesh=mesh, in_specs=(both,) * 5, out_specs=both, check_vma=False,
    )
```

```python
import functools
import math

import jax
import jax.numpy as jnp
from jax import lax
from jax.experimental import pallas as pl
from jax.experimental.pallas import tpu as pltpu
from jax.sharding import PartitionSpec as P

MESH = pl.DeviceIdType.MESH
REACH = 2
NY = 4
DEPTHS = (2, 2, 2, 2)
NT = (((1,), (1,)), ((), ()))
F32 = jnp.float32
BF16 = jnp.bfloat16


def dot(a, b):
    return jnp.dot(a, b, preferred_element_type=F32)


def dot_nt(a, b):
    return lax.dot_general(a, b, NT, preferred_element_type=F32)


def wrap(value, size):
    return jnp.where(value >= size, value - size, value)


def around(offset, size):
    return min(offset, size - offset)


def tree_sum(terms):
    while len(terms) > 1:
        terms = [sum(terms[i : i + 2][1:], terms[i]) for i in range(0, len(terms), 2)]
    return terms[0]


def front_kernel(
    dims,
    cols_hbm, aff_hbm, basis_hbm, deg_hbm, reorder_hbm,
    gram_out, perm_out,
    cols, aff, basis, deg, reorder, halo, halo_deg, ext, iroot, parts,
    gpack, rs_buf, z_src, z_buf, ag_src, ag_buf,
    in_sem, aff_sem, halo_send, halo_recv, rs_send, rs_recv, z_send, z_recv, ag_send, ag_recv, plane_sem, far_sem,
):
    nz, ny, ns, count, block = dims
    nx = ns // 2
    plane = ny * nx
    total = ny * nz * ns
    rank = basis.shape[0]
    row, sub = lax.axis_index("rows"), lax.axis_index("sub")
    y, z = row // nz, row % nz
    x, core = sub // 2, sub % 2
    mine = y * nx + x
    linear = row * ns + sub

    up, down = wrap(linear + 1, total), wrap(linear + total - 1, total)
    right = (up // ns, up % ns)
    left = (down // ns, down % ns)
    ys = [wrap(y + d, ny) for d in range(ny)]
    xs = [wrap(x + d, nx) for d in range(nx)]
    plane_offsets = sorted(
        ((dy, dx) for dy in range(ny) for dx in range(nx) if dy or dx),
        key=lambda o: -(around(o[0], ny) + around(o[1], nx)))
    plane_ids = [(ys[dy] * nz + z, 2 * xs[dx] + core) for dy, dx in plane_offsets]
    rs_targets = [
        ((ys[dy] * nz + z, 2 * xs[dx] + c), ys[dy] * nx + xs[dx])
        for dy, dx in plane_offsets for c in (core, 1 - core)]
    partner = (row, 2 * x + 1 - core)
    rs_targets.append((partner, mine))
    z_offsets = sorted(range(1, nz), key=lambda d: -around(d, nz))
    z_ids = [(y * nz + wrap(z + d, nz), sub) for d in z_offsets]
    y_line = [(ys[d] * nz + z, sub) for d in range(1, ny)]
    x_line = [partner] + [(row, 2 * xs[d] + c) for d in range(1, nx) for c in (core, 1 - core)]

    def z_id(d):
        return (y * nz + wrap(z + d, nz), sub)

    near = max(1, nz // 8)
    steps = [near, 2 * near]
    z_line = [z_id(d) for d in range(1, nz) if around(d, nz) <= near]

    barrier = pltpu.get_barrier_semaphore()

    def signal(device):
        pl.semaphore_signal(barrier, inc=1, device_id=device, device_id_type=MESH)

    def remote(src, dst, send, recv, device):
        return pltpu.make_async_remote_copy(
            src, dst, send, recv, device_id=device, device_id_type=MESH)

    def drain(ref, sem):
        pltpu.make_async_copy(ref, ref, sem).wait()

    signal(left)
    signal(right)

    deg_in = pltpu.make_async_copy(deg_hbm, deg, in_sem.at[0])
    basis_in = pltpu.make_async_copy(basis_hbm, basis, in_sem.at[1])
    cols_in = pltpu.make_async_copy(cols_hbm, cols, in_sem.at[2])
    reorder_in = pltpu.make_async_copy(reorder_hbm, reorder, in_sem.at[3])

    def aff_in(b):
        return pltpu.make_async_copy(aff_hbm.at[b], aff.at[b], aff_sem.at[b])

    inner = tuple(range(REACH, count - REACH))
    outer = tuple(range(REACH)) + tuple(range(count - REACH, count))
    deg_in.start()
    basis_in.start()
    cols_in.start()
    for b in inner:
        aff_in(b).start()
    for device in x_line + y_line + z_line:
        signal(device)
    for b in outer:
        aff_in(b).start()
    reorder_in.start()

    pl.semaphore_wait(barrier, 2 + len(x_line) + len(y_line) + len(z_line))

    width = REACH * block
    pieces = deg.shape[0]
    sends = [
        remote(basis.at[:, pl.ds((count - REACH) * block, width)], halo.at[0],
               halo_send.at[0], halo_recv.at[0], right),
        remote(basis.at[:, pl.ds(0, width)], halo.at[1],
               halo_send.at[1], halo_recv.at[1], left),
        remote(deg_hbm.at[pieces - 1], halo_deg.at[0], halo_send.at[2], halo_recv.at[2], right),
        remote(deg_hbm.at[0], halo_deg.at[1], halo_send.at[3], halo_recv.at[3], left),
    ]
    basis_in.wait()
    for copy in sends:
        copy.start()

    def tell(sem, devices):
        for device in devices:
            pl.semaphore_signal(sem, inc=1, device_id=device, device_id_type=MESH)

    tell(plane_sem, y_line)
    tell(far_sem.at[0], [z_id(steps[0]), z_id(nz - steps[0])])

    def spread(root, first_row):
        return jnp.concatenate(
            [root[first_row + h : first_row + h + 1, :] for h in range(block // 128)], axis=1)

    def scaled(raw, factor):
        return (raw.astype(F32) * factor).astype(BF16)

    per_block = block // 128
    deg_in.wait()
    for g in range(pieces):
        root = lax.rsqrt(deg[g].astype(F32))
        for j in range(REACH):
            iroot[g * REACH + j] = spread(root, j * per_block)
    for b in range(count):
        ext[b + REACH] = scaled(basis[:, b * block : (b + 1) * block], iroot[b])
    cols_in.wait()

    first = linear * count

    def place(k, b):
        return cols[k, b] - first + REACH

    def fetch(slot, low, high):
        return ext[jnp.clip(slot, low, high)]

    here = (REACH, count + REACH - 1)
    anyone = (0, count + 2 * REACH - 1)

    def split(b, acc):
        image = acc * iroot[b]
        hi = image.astype(BF16)
        rest = image - hi.astype(F32)
        mid = rest.astype(BF16)
        lo = (rest - mid.astype(F32)).astype(BF16)
        parts[b, :rank, :] = hi
        parts[b, rank:, :] = mid
        return hi, mid, lo

    def gram_of(splits):
        hi, mid, lo = (jnp.concatenate(p, axis=1) for p in zip(*splits))
        g1 = dot_nt(jnp.concatenate([hi, mid, lo], axis=0), hi)
        g2 = dot_nt(jnp.concatenate([hi, mid], axis=0), mid)
        g3 = dot_nt(hi, lo)
        small = g1[2 * rank :] + g2[rank:] + g3
        cross = g1[rank : 2 * rank] + g2[:rank]
        return g1[:rank] + (cross + small)

    for b in inner:
        aff_in(b).wait()
    splits = []
    for b in inner:
        acc = dot_nt(ext[b + REACH], aff[b, 0])
        for k in range(1, 3):
            acc += dot_nt(fetch(place(k, b), *here), aff[b, k])
        splits.append(split(b, acc))
    gram = gram_of(splits)
    for b in outer:
        aff_in(b).wait()
    starts, pending = [], []
    for b in outer:
        acc = dot_nt(ext[b + REACH], aff[b, 0])
        one, two = place(1, b), place(2, b)
        if b in (REACH - 1, count - REACH):
            away = (one < here[0]) | (one > here[1])
            acc += dot_nt(fetch(jnp.where(away, two, one), *here), aff[b, jnp.where(away, 2, 1)])
            pending.append([(jnp.where(away, one, two), jnp.where(away, 1, 2))])
        else:
            pending.append([(one, 1), (two, 2)])
        starts.append(acc)

    pl.semaphore_wait(far_sem.at[0], 2)
    tell(far_sem.at[1], [z_id(steps[1]), z_id(nz - steps[1])])
    for copy in sends:
        copy.wait_recv()
    for side, base in ((0, 0), (1, count + REACH)):
        root = lax.rsqrt(halo_deg[side].astype(F32))
        for j in range(REACH):
            ext[base + j] = scaled(
                halo[side, :, j * block : (j + 1) * block], spread(root, j * per_block))

    splits = []
    for b, acc, terms in zip(outer, starts, pending):
        for slot, k in terms:
            acc += dot_nt(fetch(slot, *anyone), aff[b, k])
        splits.append(split(b, acc))
    gram += gram_of(splits)

    half = rank // 2
    packed = jnp.concatenate([gram[:half], gram[half:]], axis=1)
    per = half // plane
    for q in range(plane):
        gpack[q] = packed[q * per : (q + 1) * per]

    if y_line:
        pl.semaphore_wait(plane_sem, len(y_line))
    for i, (device, q) in enumerate(rs_targets):
        remote(gpack.at[q], rs_buf.at[i], rs_send, rs_recv, device).start()

    reorder_in.wait()
    ids = lax.broadcasted_iota(jnp.int32, (block, block), 0)
    for b in range(count):
        pick = jnp.where(ids == reorder[b : b + 1, :], 1.0, 0.0).astype(BF16)
        perm_out[b] = dot(parts[b], pick).astype(BF16)

    drain(rs_buf, rs_recv)
    pl.semaphore_wait(far_sem.at[1], 2)
    z_src[...] = tree_sum([gpack[mine]] + [rs_buf[i] for i in range(len(rs_targets))])
    for i, device in enumerate(z_ids):
        remote(z_src, z_buf.at[i], z_send, z_recv, device).start()
    for copy in sends:
        copy.wait_send()
    drain(rs_buf, rs_send)

    drain(z_buf, z_recv)
    chunk = tree_sum([z_src[...]] + [z_buf[i] for i in range(nz - 1)])
    ag_src[...] = chunk
    ag_buf[mine] = chunk
    for device in plane_ids:
        remote(ag_src, ag_buf.at[mine], ag_send, ag_recv, device).start()
    drain(z_buf, z_send)
    drain(ag_buf.at[pl.ds(0, plane - 1)], ag_send)
    drain(ag_buf.at[pl.ds(0, plane - 1)], ag_recv)
    for q in range(plane):
        gram_out[q * per : (q + 1) * per] = ag_buf[q]


def back_kernel(scale, gram_ref, perm, out_hbm, out, out_sem):
    count, depth, block = perm.shape
    rank = depth // 2
    half = rank // 2
    tiles = rank // 8

    packed = gram_ref[...]
    low = pltpu.roll(packed, rank, 1)
    lane = lax.broadcasted_iota(jnp.int32, (8, 2 * rank), 1)
    sublane = lax.broadcasted_iota(jnp.int32, (8, 2 * rank), 0)
    state = []
    for t in range(tiles):
        source = low if t < tiles // 2 else packed
        r = (8 * t) % half
        eye = jnp.where(lane == sublane + 8 * t, 1.0, 0.0)
        state.append(jnp.where(lane < rank, eye, source[r : r + 8]))

    def row(v, j):
        return jnp.broadcast_to(v[j : j + 1, :], v.shape)

    rows = []
    start = 0
    for depth in DEPTHS:
        span = range(start, tiles)
        cols = []
        for j in range(8 * depth):
            k = rank + 8 * start + j
            cols.append({v: jnp.broadcast_to(state[v][:, k : k + 1], (8, 2 * rank))
                         for v in span if v >= start + j // 8})
        mults = []
        pivot_rows = []
        pivots = [None] * depth
        for j in range(8 * depth):
            t, i = start + j // 8, j % 8
            pivot = row(cols[j][t], i)
            d = j // 8
            pivots[d] = pivot if i == 0 else jnp.where(sublane == i, pivot, pivots[d])
            inv = 1.0 / pivot
            mult = {v: c * inv for v, c in cols[j].items()}
            for jj in range(j + 1, 8 * depth):
                top = row(cols[j][start + jj // 8], jj % 8)
                cols[jj] = {v: c - mult[v] * top for v, c in cols[jj].items()}
            mult[t] = jnp.where(sublane > i, mult[t], 0.0)
            pivot_row = row(state[t], i)
            for v in range(t, start + depth):
                state[v] = state[v] - mult[v] * pivot_row
            mults.append(mult)
            pivot_rows.append(pivot_row)
        for v in range(start + depth, tiles):
            for mult, pivot_row in zip(mults, pivot_rows):
                state[v] = state[v] - mult[v] * pivot_row
        for d in range(depth):
            rows.append(state[start + d] * (lax.rsqrt(pivots[d]) * scale))
        start += depth

    inverse = jnp.concatenate(rows, axis=0)[:, :rank]
    hi = inverse.astype(BF16)
    mid = (inverse - hi.astype(F32)).astype(BF16)
    left = jnp.concatenate(
        [jnp.concatenate([hi, hi], axis=1), jnp.concatenate([mid, mid], axis=1)], axis=0)

    def out_copy(b):
        cols = pl.ds(b * block, block)
        return pltpu.make_async_copy(out.at[:, cols], out_hbm.at[:, cols], out_sem.at[b])

    for b in range(count):
        both = dot(left, perm[b])
        out[:, b * block : (b + 1) * block] = both[:rank] + both[rank:]
        out_copy(b).start()
    for b in range(count):
        out_copy(b).wait()


def body(ny, nz, ns, affinity, old_basis, degrees, column_blocks, reorder):
    count, _, block, _ = affinity.shape
    rows_here, rank = old_basis.shape
    plane = ny * (ns // 2)
    per = rank // 2 // plane
    anywhere = pl.BlockSpec(memory_space=pl.ANY)
    vmem = pl.BlockSpec(memory_space=pltpu.VMEM)
    dma = pltpu.SemaphoreType.DMA
    width = REACH * block // 128
    gram, perm = pl.pallas_call(
        functools.partial(front_kernel, (nz, ny, ns, count, block)),
        name="front",
        out_shape=(
            pltpu.VMEM((rank // 2, 2 * rank), F32),
            pltpu.VMEM((count, 2 * rank, block), BF16),
        ),
        in_specs=[anywhere] * 5,
        out_specs=(vmem, vmem),
        scratch_shapes=[
            pltpu.SMEM(column_blocks.shape[::-1], jnp.int32),
            pltpu.VMEM(affinity.shape, BF16),
            pltpu.VMEM((rank, rows_here), BF16),
            pltpu.VMEM((count // REACH, width, 128), jnp.int32),
            pltpu.VMEM(reorder.shape, jnp.int32),
            pltpu.VMEM((2, rank, REACH * block), BF16),
            pltpu.VMEM((2, width, 128), jnp.int32),
            pltpu.VMEM((count + 2 * REACH, rank, block), BF16),
            pltpu.VMEM((count, 1, block), F32),
            pltpu.VMEM((count, 2 * rank, block), BF16),
            pltpu.VMEM((plane, per, 2 * rank), F32),
            pltpu.VMEM((2 * plane - 1, per, 2 * rank), F32),
            pltpu.VMEM((per, 2 * rank), F32),
            pltpu.VMEM((nz - 1, per, 2 * rank), F32),
            pltpu.VMEM((per, 2 * rank), F32),
            pltpu.VMEM((plane, per, 2 * rank), F32),
            dma((4,)), dma((count,)), dma((4,)), dma((4,)),
            dma, dma, dma, dma, dma, dma,
            pltpu.SemaphoreType.REGULAR, pltpu.SemaphoreType.REGULAR((2,)),
        ],
        compiler_params=pltpu.CompilerParams(collective_id=0, has_side_effects=True),
    )(column_blocks.T, affinity, old_basis.T, degrees.reshape(-1, width, 128), reorder)
    items = rows_here * lax.axis_size("rows") * lax.axis_size("sub")
    out = pl.pallas_call(
        functools.partial(back_kernel, math.sqrt(items)),
        name="back",
        out_shape=jax.ShapeDtypeStruct((rank, rows_here), F32),
        in_specs=[vmem, vmem],
        out_specs=anywhere,
        scratch_shapes=[pltpu.VMEM((rank, rows_here), F32), dma((count,))],
    )(*(pltpu.with_memory_space_constraint(a, pltpu.VMEM) for a in (gram, perm)))
    return out.T


def solution(mesh):
    rows, ns = mesh.shape["rows"], mesh.shape["sub"]
    nz = rows // NY
    both = P(("rows", "sub"))
    return jax.shard_map(
        functools.partial(body, rows // nz, nz, ns),
        mesh=mesh, in_specs=(both,) * 5, out_specs=both, check_vma=False,
    )
```
